32 devices in a mesh: gy: 8 (over y, x, core), gz: 4 (over z).
Axes of the slice: x: 2, y: 2, z: 4, core: 2. Of those that a mesh axis runs over, the one named last changes fastest.
Arguments:
- initial_warmth: float32 [1024, 32, 512], P('gy', None, 'gz'), may hold values from -18 to 18
- transverse_factor: float32 [32, 512], P(None, 'gz'), may hold values from 0.05 to 0.24
- energy_supply_series: float32 [1024, 32, 512], P('gy', None, 'gz'), may hold values from -1.5 to 1.5
Outputs:
- temperature_next: float32 [1024, 32, 512], P('gy', None, 'gz')
The draws below stay inside these ranges and needn't reach their ends.
All inputs are finite; a program needn't handle non-finite values.
Results may differ from the reference program's by a relative error of at most 0.0001.
Values sent between devices are 32-bit elements; how exact they have to be, the bound alone decides.
A program may use at most 64 MiB of HBM per device.

```python
import math
import jax
import jax.numpy as jnp
from jax import lax

NODES_ACROSS_EAST = 1024
UPWARD_SHARD = 128
ITERATION_TOTAL = 2
NODES_NORTHWARD = 32
NODES_UPWARD = 512


def draw_energy_supply_series(key, part):
    return jnp.clip(0.3 * jax.random.normal(key, (NODES_ACROSS_EAST, NODES_NORTHWARD, NODES_UPWARD), jnp.float32), -1.5, 1.5)


def levels(stream_key, shape, shards, low, largest):
    gain = 1.0
    for position, shards_of in shards:
        draws = jax.random.uniform(jax.random.fold_in(jax.random.fold_in(stream_key, 6), position), (shards_of,), jnp.float32, low / len(shards), largest / len(shards))
        gain = gain * jnp.repeat(jnp.exp(draws), shape[position] // shards_of).reshape((-1,) + (1,) * (len(shape) - 1 - position))
    return gain


def normal_values(key, dims, scale, most, pieces=(), kind=jnp.bfloat16):
    result = jax.random.normal(key, dims, jnp.float32) * scale
    if len(pieces) > 0:
        result = levels(key, dims, pieces, -0.22, 0.18) * result
    return jnp.clip(result, min=-most, max=most).astype(kind)


def setup_inputs(seed: int = 0) -> dict:
    seeds = jax.random.split(jax.random.key(seed), 4)
    return {
        "initial_warmth": normal_values(seeds[0], (NODES_ACROSS_EAST, NODES_NORTHWARD, NODES_UPWARD), 3.0, 18.0, ((0, 8), (2, 4)), jnp.float32),
        "transverse_factor": jnp.clip(jnp.exp(math.log(0.24) - 1.5686159 * jax.random.uniform(seeds[1], (NODES_NORTHWARD, NODES_UPWARD), jnp.float32) ** levels(seeds[1], (NODES_NORTHWARD, NODES_UPWARD), ((1, 4),), -0.2, 0.2)), 0.05, 0.24),
        "energy_supply_series": draw_energy_supply_series(jax.random.fold_in(seeds[3], 71), 0),
    }


coupling = 400.0


def reference(initial_warmth, transverse_factor, energy_supply_series):
    waves = jnp.arange(NODES_ACROSS_EAST // 2 + 1).astype(jnp.float32)
    eigenvalue = 1.0 + 4.0 * coupling * jnp.sin(jnp.pi * waves / NODES_ACROSS_EAST) ** 2
    column_groups = NODES_UPWARD // UPWARD_SHARD

    def solve_block(block):
        spectrum = jnp.fft.rfft(block, axis=0)
        return jnp.fft.irfft(spectrum / eigenvalue[:, None, None], n=NODES_ACROSS_EAST, axis=0).astype(jnp.float32)

    def advance_solution(single_update, warmth_field):
        gathered_columns = jnp.moveaxis(warmth_field.reshape(NODES_ACROSS_EAST, NODES_NORTHWARD, column_groups, UPWARD_SHARD), 2, 0)
        backward_euler_solve = jnp.moveaxis(lax.map(solve_block, gathered_columns), 0, 2).reshape(NODES_ACROSS_EAST, NODES_NORTHWARD, NODES_UPWARD)
        second_difference = jnp.roll(backward_euler_solve, 1, 1) + jnp.roll(backward_euler_solve, -1, 1)
        second_difference = second_difference + jnp.roll(backward_euler_solve, 1, 2) + jnp.roll(backward_euler_solve, -1, 2) - 4.0 * backward_euler_solve
        return backward_euler_solve + transverse_factor[None] * second_difference + energy_supply_series

    return lax.fori_loop(0, ITERATION_TOTAL, advance_solution, initial_warmth)
```

```python
import jax
import jax.numpy as jnp
import numpy as np
from jax import lax
from jax.sharding import PartitionSpec as P

coupling = 400.0


def tables(m, parts):
    root = (1.0 + 2.0 * coupling - np.sqrt(1.0 + 4.0 * coupling)) / (2.0 * coupling)
    height = 1.0 / (1.0 + 2.0 * coupling - 2.0 * coupling * root)
    delta = (1.0 + root**2) / (1.0 - root**2)
    cell = np.arange(m)
    distance = np.abs(cell[:, None] - cell[None, :])
    local = np.concatenate(
        [height**2 * (delta + distance) * root**distance, height * root**distance], axis=1
    )
    rows = []
    for reach in (m - 1 - cell, cell):
        fall = root**reach
        rows.append(np.concatenate([height**2 * fall, 0.0 * fall]))
        rows.append(np.concatenate([height**2 * (delta + reach) * fall, height * fall]))
    sums = np.stack(rows)
    step = root**m
    whole = step**parts
    mix = np.zeros((parts, 4, parts, 4))
    for d in range(parts):
        for p in range(1, parts + 1):
            near = step ** (p - 1) / (1.0 - whole)
            far = m * step ** (p - 1) * (
                (p - 1) / (1.0 - whole) + parts * whole / (1.0 - whole) ** 2
            )
            for first, other in ((0, (d - p) % parts), (2, (d + p) % parts)):
                mix[d, first, other, first] = near
                mix[d, first + 1, other, first + 1] = near
                mix[d, first + 1, other, first] = far
    columns = []
    for reach in (cell + 1, m - cell):
        columns += [reach * root**reach, root**reach]
    spread = np.stack(columns, axis=1)
    return [t.astype(np.float32) for t in (local, sums, mix, spread)]


def shifted(block, axis, by):
    count = lax.axis_size(axis)
    return lax.ppermute(block, axis, [(i, (i + by) % count) for i in range(count)])


def transverse(wide, c):
    mid = wide[..., 1:-1]
    around = jnp.roll(mid, 1, -2) + jnp.roll(mid, -1, -2) + wide[..., 2:] + wide[..., :-2]
    return mid + c * (around - 4.0 * mid)


def per_device(field, c, q):
    m, ny, nz = field.shape
    parts = lax.axis_size("gy")
    local, sums, mix, spread = tables(m, parts)

    def edges(a, b, at):
        planes = [field[:, :, a], field[:, :, b], q[:, :, at]]
        return jnp.concatenate(planes + [c[None, :, at]], axis=0)

    low = shifted(edges(nz - 2, nz - 1, nz - 1), "gz", 1)
    high = shifted(edges(1, 0, 0), "gz", -1)

    def plane(packed, k):
        return packed[k * m : (k + 1) * m, :, None]

    wide_field = jnp.concatenate(
        [plane(low, 0), plane(low, 1), field, plane(high, 1), plane(high, 0)], axis=2
    )
    wide_q = jnp.concatenate([plane(low, 2), q, plane(high, 2)], axis=2)
    wide_c = jnp.concatenate([low[3 * m, :, None], c, high[3 * m, :, None]], axis=1)
    g = transverse(transverse(wide_field, wide_c), c)
    h = transverse(wide_q, c)
    both = jnp.concatenate([g, h], axis=0)

    def dot(a, b):
        return lax.dot_general(
            a, b, (((1,), (0,)), ((), ())), precision=lax.Precision.HIGH,
            preferred_element_type=jnp.float32,
        )

    planes = dot(jnp.asarray(sums), both)
    gathered = lax.all_gather(planes, "gy", axis=0, tiled=True)
    mine = lax.dynamic_index_in_dim(
        jnp.asarray(mix.reshape(parts, 4, parts * 4)), lax.axis_index("gy"), 0, False
    )
    incoming = dot(mine, gathered)
    return dot(jnp.asarray(local), both) + dot(jnp.asarray(spread), incoming) + q


def solution(mesh):
    placed = (P("gy", None, "gz"), P(None, "gz"), P("gy", None, "gz"))
    return jax.shard_map(
        per_device, mesh=mesh, in_specs=placed, out_specs=P("gy", None, "gz"), check_vma=False
    )
```

```python
import functools

import jax
import jax.numpy as jnp
import numpy as np
from jax import lax
from jax.experimental import pallas as pl
from jax.experimental.pallas import tpu as pltpu
from jax.sharding import PartitionSpec as P

coupling = 400.0
LANES = 128
PACK = 32
UNROLL = 4


def constants(m, parts):
    root = (1.0 + 2.0 * coupling - np.sqrt(1.0 + 4.0 * coupling)) / (2.0 * coupling)
    height = 1.0 / (1.0 + 2.0 * coupling - 2.0 * coupling * root)
    step = root**m
    whole = step**parts
    near, far = {}, {}
    for p in range(1, parts + 1):
        near[p] = step ** (p - 1) / (1.0 - whole)
        far[p] = m * step ** (p - 1) * (
            (p - 1) / (1.0 - whole) + parts * whole / (1.0 - whole) ** 2
        )
    return float(root), float(height), near, far


def kernel(
    m, ny, parts, rings,
    f_hbm, c_ref, q_hbm, out_ref,
    fv, qv, hv, av, pf, to_right, to_left, from_left, from_right, d_one, d_two, d_q,
    pieces, gathered, mixed, incoming,
    load_f, load_q, z_send, z_recv, s_one, r_one, s_two, r_two,
):
    groups = m // PACK
    root, height, near, far = constants(m, parts)
    me = lax.axis_index("gy")
    mez = lax.axis_index("gz")
    right = lax.rem(mez + 1, rings)
    left = lax.rem(mez + rings - 1, rings)

    loads = []
    for k in range(groups):
        rows = pl.ds(k * PACK, PACK)
        one = pltpu.make_async_copy(f_hbm.at[rows], fv.at[rows], load_f.at[k])
        two = pltpu.make_async_copy(q_hbm.at[rows], qv.at[rows], load_q.at[k])
        one.start()
        two.start()
        loads.append((one, two))

    barrier = pltpu.get_barrier_semaphore()
    for z in (left, right):
        pl.semaphore_signal(
            barrier, inc=1, device_id={"gz": z}, device_id_type=pl.DeviceIdType.MESH
        )
    for o in range(1, parts):
        pl.semaphore_signal(
            barrier, inc=1, device_id={"gy": lax.rem(me + o, parts)},
            device_id_type=pl.DeviceIdType.MESH,
        )

    c = c_ref[...]
    lane = lax.broadcasted_iota(jnp.int32, (ny, LANES), 1)
    slot = lane % 4
    owner = lane // 4
    zero = jnp.zeros((ny, LANES), jnp.float32)

    def roll(v, by):
        return pltpu.roll(v, by, 1)

    def c_step(j, packed):
        return jnp.where(owner == j, roll(c, 4 * j + 2), packed)

    pc = lax.fori_loop(0, PACK, c_step, zero)
    c_right = roll(pc, 2)
    c_left = roll(pc, LANES - 2)

    sends = []
    for k in range(groups):
        loads[k][0].wait()
        loads[k][1].wait()

        def pack_step(i, carry):
            a, b = carry
            for u in range(UNROLL):
                j = i * UNROLL + u
                hit = owner == j
                a = jnp.where(hit, roll(fv[k * PACK + j], 4 * j + 2), a)
                b = jnp.where(hit, roll(qv[k * PACK + j], 4 * j + 3), b)
            return a, b

        a, b = lax.fori_loop(0, PACK // UNROLL, pack_step, (zero, zero))
        pf[k] = a
        to_right[k] = jnp.where(slot < 2, a, jnp.where(slot == 2, b, c_right))
        to_left[k] = jnp.where(
            slot >= 2, a, jnp.where(slot == 1, roll(b, LANES - 2), c_left)
        )
        if k == 0:
            pl.semaphore_wait(barrier, parts + 1)
        for side, (source, landing, z) in enumerate(
            ((to_right, from_left, right), (to_left, from_right, left))
        ):
            copy = pltpu.make_async_remote_copy(
                src_ref=source.at[k], dst_ref=landing.at[k],
                send_sem=z_send.at[side, k], recv_sem=z_recv.at[side, k],
                device_id={"gz": z}, device_id_type=pl.DeviceIdType.MESH,
            )
            copy.start()
            sends.append(copy)
    for copy in sends:
        copy.wait()

    def across(v):
        return pltpu.roll(v, 1, 0) + pltpu.roll(v, ny - 1, 0)

    c_low = jnp.where(slot < 2, roll(from_left[0], LANES - 2), pc)
    c_high = jnp.where(slot < 2, pc, roll(from_right[0], 2))
    for k in range(groups):
        lo, hi, own = from_left[k], from_right[k], pf[k]

        def update(v, factor):
            return v + factor * (across(v) + roll(v, 1) + roll(v, LANES - 1) - 4.0 * v)

        low = update(jnp.where(slot < 2, lo, own), c_low)
        high = update(jnp.where(slot < 2, own, hi), c_high)
        d_one[k] = jnp.where(slot == 1, roll(hi, LANES - 1), roll(lo, 1))
        d_two[k] = jnp.where(slot == 1, roll(high, LANES - 1), roll(low, 1))
        d_q[k] = jnp.where(slot == 1, hi, lo)

    first = lane == 0
    last = lane == LANES - 1

    def transverse(v, edge):
        below = jnp.where(first, edge, roll(v, 1))
        above = jnp.where(last, edge, roll(v, LANES - 1))
        return v + c * (across(v) + below + above - 4.0 * v)

    carry = zero
    for k in range(groups):
        packed = (d_one[k], d_two[k], d_q[k])

        def forward(i, a):
            for u in range(UNROLL):
                j = i * UNROLL + u
                x = k * PACK + j
                one, two, three = (roll(d, LANES - 2 - 4 * j) for d in packed)
                g = transverse(transverse(fv[x], one), two)
                hv[x] = transverse(qv[x], three)
                fv[x] = g
                a = root * a + g
                av[x] = a
            return a

        carry = lax.fori_loop(0, PACK // UNROLL, forward, carry)
    sum_low = carry

    def backward(i, carry):
        pull, pull_two, ahead, weight = carry
        for u in range(UNROLL):
            x = m - 1 - (i * UNROLL + u)
            b = root * pull
            w = height * (av[x] + b) + hv[x]
            pull = b + fv[x]
            b_two = root * pull_two
            hv[x] = w
            av[x] = b_two
            pull_two = b_two + w
            ahead = ahead + weight * w
            weight = weight * root
        return pull, pull_two, ahead, weight

    sum_high, twice_high, twice_low, _ = lax.fori_loop(
        0, m // UNROLL, backward, (zero, zero, zero, zero + 1.0)
    )
    same = height**2 * root**2 / (1.0 - root**2)
    cross = height**2 * root ** (m + 1) / (1.0 - root**2)
    planes = (
        (height**2 * sum_low, height * twice_low + same * sum_low + cross * sum_high),
        (height**2 * sum_high, height * twice_high + same * sum_high + cross * sum_low),
    )
    half = parts // 2
    rows = ny // half
    for way in range(2):
        for e in range(half):
            for n in range(2):
                pieces[way * half + e, n] = planes[way][n][e * rows : (e + 1) * rows]

    gathered[me] = pieces[me]
    sends = []
    for o in range(1, parts):
        peer = lax.rem(me + o, parts)
        copy = pltpu.make_async_remote_copy(
            src_ref=pieces.at[peer], dst_ref=gathered.at[me],
            send_sem=s_one.at[o], recv_sem=r_one.at[o],
            device_id={"gy": peer}, device_id_type=pl.DeviceIdType.MESH,
        )
        copy.start()
        sends.append(copy)
    for copy in sends:
        copy.wait()

    from_below = me < half
    for d in range(parts):
        total_u = jnp.zeros((rows, LANES), jnp.float32)
        total_v = total_u
        for e in range(parts):
            down = (d - e) % parts or parts
            up = (e - d) % parts or parts
            by = jnp.where(from_below, near[down], near[up])
            by_far = jnp.where(from_below, far[down], far[up])
            total_u = total_u + by * gathered[e, 0]
            total_v = total_v + by * gathered[e, 1] + by_far * gathered[e, 0]
        mixed[d, 0] = total_u
        mixed[d, 1] = total_v

    incoming[me] = mixed[me]
    sends = []
    for o in range(1, parts):
        peer = lax.rem(me + o, parts)
        copy = pltpu.make_async_remote_copy(
            src_ref=mixed.at[peer], dst_ref=incoming.at[me],
            send_sem=s_two.at[o], recv_sem=r_two.at[o],
            device_id={"gy": peer}, device_id_type=pl.DeviceIdType.MESH,
        )
        copy.start()
        sends.append(copy)

    def finish_local(i, a):
        for u in range(UNROLL):
            x = i * UNROLL + u
            a = root * a + hv[x]
            av[x] = height * (a + av[x]) + qv[x]
        return a

    lax.fori_loop(0, m // UNROLL, finish_local, zero)
    for copy in sends:
        copy.wait()

    low_u, low_v, high_u, high_v = (
        jnp.concatenate([incoming[way * half + e, n] for e in range(half)], axis=0)
        for way in range(2)
        for n in range(2)
    )
    mirror = height**2 * root / (1.0 - root**2)
    low_v = low_v + mirror * sum_high
    high_v = high_v + mirror * sum_low

    def add_high(i, carry):
        u_now, v_now = carry
        for u in range(UNROLL):
            x = m - 1 - (i * UNROLL + u)
            u_now = root * u_now
            v_now = root * v_now + u_now
            av[x] = av[x] + v_now
        return u_now, v_now

    lax.fori_loop(0, m // UNROLL, add_high, (high_u, high_v))

    def add_low(i, carry):
        u_now, v_now = carry
        for u in range(UNROLL):
            x = i * UNROLL + u
            u_now = root * u_now
            v_now = root * v_now + u_now
            out_ref[x] = av[x] + v_now
        return u_now, v_now

    lax.fori_loop(0, m // UNROLL, add_low, (low_u, low_v))


def per_device(field, c, q):
    m, ny, nz = field.shape
    parts = lax.axis_size("gy")
    rings = lax.axis_size("gz")
    assert nz == LANES and m % PACK == 0 and ny % (parts // 2) == 0
    groups = m // PACK
    rows = ny // (parts // 2)
    block = pltpu.VMEM((m, ny, nz), jnp.float32)
    packed = pltpu.VMEM((groups, ny, LANES), jnp.float32)
    small = pltpu.VMEM((parts, 2, rows, LANES), jnp.float32)
    dma = pltpu.SemaphoreType.DMA
    return pl.pallas_call(
        functools.partial(kernel, m, ny, parts, rings),
        out_shape=jax.ShapeDtypeStruct(field.shape, jnp.float32),
        in_specs=[
            pl.BlockSpec(memory_space=pltpu.HBM),
            pl.BlockSpec(memory_space=pltpu.VMEM),
            pl.BlockSpec(memory_space=pltpu.HBM),
        ],
        out_specs=pl.BlockSpec(memory_space=pltpu.VMEM),
        scratch_shapes=[block] * 4 + [packed] * 8 + [small] * 4 + [
            dma((groups,)), dma((groups,)), dma((2, groups)), dma((2, groups)),
            dma((parts,)), dma((parts,)), dma((parts,)), dma((parts,)),
        ],
        compiler_params=pltpu.CompilerParams(
            collective_id=0, has_side_effects=True, vmem_limit_bytes=28 * 2**20
        ),
    )(field, c, q)


def solution(mesh):
    placed = (P("gy", None, "gz"), P(None, "gz"), P("gy", None, "gz"))
    return jax.shard_map(
        per_device, mesh=mesh, in_specs=placed, out_specs=P("gy", None, "gz"), check_vma=False
    )
```

```python
import functools

import jax
import jax.numpy as jnp
import numpy as np
from jax import lax
from jax.experimental import pallas as pl
from jax.experimental.pallas import tpu as pltpu
from jax.sharding import PartitionSpec as P

coupling = 400.0
LANES = 128
PACK = 32
UNROLL = 4


def constants(m, parts):
    root = (1.0 + 2.0 * coupling - np.sqrt(1.0 + 4.0 * coupling)) / (2.0 * coupling)
    height = 1.0 / (1.0 + 2.0 * coupling - 2.0 * coupling * root)
    step = root**m
    whole = step**parts
    near, far = {}, {}
    for p in range(1, parts + 1):
        near[p] = step ** (p - 1) / (1.0 - whole)
        far[p] = m * step ** (p - 1) * (
            (p - 1) / (1.0 - whole) + parts * whole / (1.0 - whole) ** 2
        )
    return float(root), float(height), near, far


def kernel(
    m, ny, parts, rings,
    f_hbm, c_ref, q_hbm, out_ref,
    fv, qv, hv, av, pf, to_right, to_left, from_left, from_right, d_one, d_two, d_q,
    pieces, gathered, mixed, incoming,
    load_f, load_q, z_send, z_recv, s_one, r_one, s_two, r_two,
):
    groups = m // PACK
    root, height, near, far = constants(m, parts)
    me = lax.axis_index("gy")
    mez = lax.axis_index("gz")
    right = lax.rem(mez + 1, rings)
    left = lax.rem(mez + rings - 1, rings)

    loads = []
    for k in range(groups):
        rows = pl.ds(k * PACK, PACK)
        one = pltpu.make_async_copy(f_hbm.at[rows], fv.at[rows], load_f.at[k])
        two = pltpu.make_async_copy(q_hbm.at[rows], qv.at[rows], load_q.at[k])
        one.start()
        two.start()
        loads.append((one, two))

    barrier = pltpu.get_barrier_semaphore()
    for z in (left, right):
        pl.semaphore_signal(
            barrier, inc=1, device_id={"gz": z}, device_id_type=pl.DeviceIdType.MESH
        )
    for o in range(1, parts):
        pl.semaphore_signal(
            barrier, inc=1, device_id={"gy": lax.rem(me + o, parts)},
            device_id_type=pl.DeviceIdType.MESH,
        )

    c = c_ref[...]
    lane = lax.broadcasted_iota(jnp.int32, (ny, LANES), 1)
    slot = lane % 4
    owner = lane // 4
    zero = jnp.zeros((ny, LANES), jnp.float32)

    def roll(v, by):
        return pltpu.roll(v, by, 1)

    def c_step(j, packed):
        return jnp.where(owner == j, roll(c, 4 * j + 2), packed)

    pc = lax.fori_loop(0, PACK, c_step, zero)
    c_right = roll(pc, 2)
    c_left = roll(pc, LANES - 2)

    sends = []
    for k in range(groups):
        loads[k][0].wait()
        loads[k][1].wait()

        def pack_step(i, carry):
            a, b = carry
            for u in range(UNROLL):
                j = i * UNROLL + u
                hit = owner == j
                a = jnp.where(hit, roll(fv[k * PACK + j], 4 * j + 2), a)
                b = jnp.where(hit, roll(qv[k * PACK + j], 4 * j + 3), b)
            return a, b

        a, b = lax.fori_loop(0, PACK // UNROLL, pack_step, (zero, zero))
        pf[k] = a
        to_right[k] = jnp.where(slot < 2, a, jnp.where(slot == 2, b, c_right))
        to_left[k] = jnp.where(
            slot >= 2, a, jnp.where(slot == 1, roll(b, LANES - 2), c_left)
        )
        if k == 0:
            pl.semaphore_wait(barrier, parts + 1)
        for side, (source, landing, z) in enumerate(
            ((to_right, from_left, right), (to_left, from_right, left))
        ):
            copy = pltpu.make_async_remote_copy(
                src_ref=source.at[k], dst_ref=landing.at[k],
                send_sem=z_send.at[side, k], recv_sem=z_recv.at[side, k],
                device_id={"gz": z}, device_id_type=pl.DeviceIdType.MESH,
            )
            copy.start()
            sends.append(copy)
    for copy in sends:
        copy.wait()

    def across(v):
        return pltpu.roll(v, 1, 0) + pltpu.roll(v, ny - 1, 0)

    c_low = jnp.where(slot < 2, roll(from_left[0], LANES - 2), pc)
    c_high = jnp.where(slot < 2, pc, roll(from_right[0], 2))
    for k in range(groups):
        lo, hi, own = from_left[k], from_right[k], pf[k]

        def update(v, factor):
            return v + factor * (across(v) + roll(v, 1) + roll(v, LANES - 1) - 4.0 * v)

        low = update(jnp.where(slot < 2, lo, own), c_low)
        high = update(jnp.where(slot < 2, own, hi), c_high)
        d_one[k] = jnp.where(slot == 1, roll(hi, LANES - 1), roll(lo, 1))
        d_two[k] = jnp.where(slot == 1, roll(high, LANES - 1), roll(low, 1))
        d_q[k] = jnp.where(slot == 1, hi, lo)

    first = lane == 0
    last = lane == LANES - 1

    def transverse(v, edge):
        below = jnp.where(first, edge, roll(v, 1))
        above = jnp.where(last, edge, roll(v, LANES - 1))
        return v + c * (across(v) + below + above - 4.0 * v)

    carry = zero
    for k in range(groups):
        packed = (d_one[k], d_two[k], d_q[k])

        def forward(i, a):
            for u in range(UNROLL):
                j = i * UNROLL + u
                x = k * PACK + j
                one, two, three = (roll(d, LANES - 2 - 4 * j) for d in packed)
                g = transverse(transverse(fv[x], one), two)
                hv[x] = transverse(qv[x], three)
                fv[x] = g
                a = root * a + g
                av[x] = a
            return a

        carry = lax.fori_loop(0, PACK // UNROLL, forward, carry)
    sum_low = carry

    def backward(i, carry):
        pull, pull_two, ahead, weight = carry
        for u in range(UNROLL):
            x = m - 1 - (i * UNROLL + u)
            b = root * pull
            w = height * (av[x] + b) + hv[x]
            pull = b + fv[x]
            b_two = root * pull_two
            hv[x] = w
            av[x] = b_two
            pull_two = b_two + w
            ahead = ahead + weight * w
            weight = weight * root
        return pull, pull_two, ahead, weight

    sum_high, twice_high, twice_low, _ = lax.fori_loop(
        0, m // UNROLL, backward, (zero, zero, zero, zero + 1.0)
    )
    same = height**2 * root**2 / (1.0 - root**2)
    cross = height**2 * root ** (m + 1) / (1.0 - root**2)
    planes = (
        (height**2 * sum_low, height * twice_low + same * sum_low + cross * sum_high),
        (height**2 * sum_high, height * twice_high + same * sum_high + cross * sum_low),
    )
    half = parts // 2
    rows = ny // half
    for way in range(2):
        for e in range(half):
            for n in range(2):
                pieces[way * half + e, n] = planes[way][n][e * rows : (e + 1) * rows]

    gathered[me] = pieces[me]
    sends = []
    for o in range(1, parts):
        peer = lax.rem(me + o, parts)
        copy = pltpu.make_async_remote_copy(
            src_ref=pieces.at[peer], dst_ref=gathered.at[me],
            send_sem=s_one.at[o], recv_sem=r_one.at[o],
            device_id={"gy": peer}, device_id_type=pl.DeviceIdType.MESH,
        )
        copy.start()
        sends.append(copy)
    for copy in sends:
        copy.wait()

    from_below = me < half
    for d in range(parts):
        total_u = jnp.zeros((rows, LANES), jnp.float32)
        total_v = total_u
        for e in range(parts):
            down = (d - e) % parts or parts
            up = (e - d) % parts or parts
            by = jnp.where(from_below, near[down], near[up])
            by_far = jnp.where(from_below, far[down], far[up])
            total_u = total_u + by * gathered[e, 0]
            total_v = total_v + by * gathered[e, 1] + by_far * gathered[e, 0]
        mixed[d, 0] = total_u
        mixed[d, 1] = total_v

    incoming[me] = mixed[me]
    sends = []
    for o in range(1, parts):
        peer = lax.rem(me + o, parts)
        copy = pltpu.make_async_remote_copy(
            src_ref=mixed.at[peer], dst_ref=incoming.at[me],
            send_sem=s_two.at[o], recv_sem=r_two.at[o],
            device_id={"gy": peer}, device_id_type=pl.DeviceIdType.MESH,
        )
        copy.start()
        sends.append(copy)

    def finish_local(i, a):
        for u in range(UNROLL):
            x = i * UNROLL + u
            a = root * a + hv[x]
            av[x] = height * (a + av[x]) + qv[x]
        return a

    lax.fori_loop(0, m // UNROLL, finish_local, zero)
    for copy in sends:
        copy.wait()

    low_u, low_v, high_u, high_v = (
        jnp.concatenate([incoming[way * half + e, n] for e in range(half)], axis=0)
        for way in range(2)
        for n in range(2)
    )
    mirror = height**2 * root / (1.0 - root**2)
    low_v = low_v + mirror * sum_high
    high_v = high_v + mirror * sum_low

    def add_high(i, carry):
        u_now, v_now = carry
        for u in range(UNROLL):
            x = m - 1 - (i * UNROLL + u)
            u_now = root * u_now
            v_now = root * v_now + u_now
            av[x] = av[x] + v_now
        return u_now, v_now

    lax.fori_loop(0, m // UNROLL, add_high, (high_u, high_v))

    def add_low(i, carry):
        u_now, v_now = carry
        for u in range(UNROLL):
            x = i * UNROLL + u
            u_now = root * u_now
            v_now = root * v_now + u_now
            out_ref[x] = av[x] + v_now
        return u_now, v_now

    lax.fori_loop(0, m // UNROLL, add_low, (low_u, low_v))


def per_device(field, c, q):
    m, ny, nz = field.shape
    parts = lax.axis_size("gy")
    rings = lax.axis_size("gz")
    assert nz == LANES and m % PACK == 0 and ny % (parts // 2) == 0
    groups = m // PACK
    rows = ny // (parts // 2)
    block = pltpu.VMEM((m, ny, nz), jnp.float32)
    packed = pltpu.VMEM((groups, ny, LANES), jnp.float32)
    small = pltpu.VMEM((parts, 2, rows, LANES), jnp.float32)
    dma = pltpu.SemaphoreType.DMA
    return pl.pallas_call(
        functools.partial(kernel, m, ny, parts, rings),
        out_shape=jax.ShapeDtypeStruct(field.shape, jnp.float32),
        in_specs=[
            pl.BlockSpec(memory_space=pltpu.HBM),
            pl.BlockSpec(memory_space=pltpu.VMEM),
            pl.BlockSpec(memory_space=pltpu.HBM),
        ],
        out_specs=pl.BlockSpec(memory_space=pltpu.VMEM),
        scratch_shapes=[block] * 4 + [packed] * 8 + [small] * 4 + [
            dma((groups,)), dma((groups,)), dma((2, groups)), dma((2, groups)),
            dma((parts,)), dma((parts,)), dma((parts,)), dma((parts,)),
        ],
        compiler_params=pltpu.CompilerParams(
            collective_id=0, has_side_effects=True, vmem_limit_bytes=28 * 2**20
        ),
    )(pltpu.with_memory_space_constraint(field, pltpu.HBM), c, pltpu.with_memory_space_constraint(q, pltpu.HBM))


def solution(mesh):
    placed = (P("gy", None, "gz"), P(None, "gz"), P("gy", None, "gz"))
    return jax.shard_map(
        per_device, mesh=mesh, in_specs=placed, out_specs=P("gy", None, "gz"), check_vma=False
    )
```

```python
import functools

import jax
import jax.numpy as jnp
import numpy as np
from jax import lax
from jax.experimental import pallas as pl
from jax.experimental.pallas import tpu as pltpu
from jax.sharding import PartitionSpec as P

coupling = 400.0
LANES = 128
PACK = 32
UNROLL = 4


def constants(m, parts):
    root = (1.0 + 2.0 * coupling - np.sqrt(1.0 + 4.0 * coupling)) / (2.0 * coupling)
    height = 1.0 / (1.0 + 2.0 * coupling - 2.0 * coupling * root)
    step = root**m
    whole = step**parts
    near, far = {}, {}
    for p in range(1, parts + 1):
        near[p] = step ** (p - 1) / (1.0 - whole)
        far[p] = m * step ** (p - 1) * (
            (p - 1) / (1.0 - whole) + parts * whole / (1.0 - whole) ** 2
        )
    return float(root), float(height), near, far


def kernel(
    m, ny, parts, rings,
    f_hbm, c_ref, q_hbm, out_ref,
    fv, qv, hv, av, pf, to_right, to_left, from_left, from_right, d_one, d_two, d_q,
    pieces, gathered, mixed, incoming,
    load_f, load_q, z_send, z_recv, s_one, r_one, s_two, r_two,
):
    groups = m // PACK
    root, height, near, far = constants(m, parts)
    me = lax.axis_index("gy")
    mez = lax.axis_index("gz")
    right = lax.rem(mez + 1, rings)
    left = lax.rem(mez + rings - 1, rings)

    loads = []
    for k in range(groups):
        rows = pl.ds(k * PACK, PACK)
        one = pltpu.make_async_copy(f_hbm.at[rows], fv.at[rows], load_f.at[k])
        two = pltpu.make_async_copy(q_hbm.at[rows], qv.at[rows], load_q.at[k])
        one.start()
        two.start()
        loads.append((one, two))

    barrier = pltpu.get_barrier_semaphore()
    for z in (left, right):
        pl.semaphore_signal(
            barrier, inc=1, device_id={"gz": z}, device_id_type=pl.DeviceIdType.MESH
        )
    for o in range(1, parts):
        pl.semaphore_signal(
            barrier, inc=1, device_id={"gy": lax.rem(me + o, parts)},
            device_id_type=pl.DeviceIdType.MESH,
        )

    c = c_ref[...]
    lane = lax.broadcasted_iota(jnp.int32, (ny, LANES), 1)
    slot = lane % 4
    owner = lane // 4
    zero = jnp.zeros((ny, LANES), jnp.float32)

    def roll(v, by):
        return pltpu.roll(v, by, 1)

    def c_step(j, packed):
        return jnp.where(owner == j, roll(c, 4 * j + 2), packed)

    pc = lax.fori_loop(0, PACK, c_step, zero)
    c_right = roll(pc, 2)
    c_left = roll(pc, LANES - 2)

    sends = []
    for k in range(groups):
        loads[k][0].wait()
        loads[k][1].wait()

        def pack_step(i, carry):
            a, b = carry
            for u in range(2 * UNROLL):
                j = i * 2 * UNROLL + u
                hit = owner == j
                a = jnp.where(hit, roll(fv[k * PACK + j], 4 * j + 2), a)
                b = jnp.where(hit, roll(qv[k * PACK + j], 4 * j + 3), b)
            return a, b

        a, b = lax.fori_loop(0, PACK // (2 * UNROLL), pack_step, (zero, zero))
        pf[k] = a
        to_right[k] = jnp.where(slot < 2, a, jnp.where(slot == 2, b, c_right))
        to_left[k] = jnp.where(
            slot >= 2, a, jnp.where(slot == 1, roll(b, LANES - 2), c_left)
        )
        if k == 0:
            pl.semaphore_wait(barrier, parts + 1)
        for side, (source, landing, z) in enumerate(
            ((to_right, from_left, right), (to_left, from_right, left))
        ):
            copy = pltpu.make_async_remote_copy(
                src_ref=source.at[k], dst_ref=landing.at[k],
                send_sem=z_send.at[side, k], recv_sem=z_recv.at[side, k],
                device_id={"gz": z}, device_id_type=pl.DeviceIdType.MESH,
            )
            copy.start()
            sends.append(copy)
    first = lane == 0
    last = lane == LANES - 1
    stay = 1.0 - 4.0 * c
    c_edge = jnp.where(first | last, c, 0.0)

    def across(v):
        return pltpu.roll(v, 1, 0) + pltpu.roll(v, ny - 1, 0)

    def transverse(v, edge):
        below = jnp.where(first, edge, roll(v, 1))
        above = jnp.where(last, edge, roll(v, LANES - 1))
        return stay * v + c * (across(v) + below + above)

    def inner(i, carry):
        for u in range(UNROLL):
            x = i * UNROLL + u
            fv[x] = transverse(fv[x], 0.0)
            hv[x] = transverse(qv[x], 0.0)
        return carry

    lax.fori_loop(0, m // UNROLL, inner, 0)

    carry = zero
    for k in range(groups):
        sends[2 * k].wait()
        sends[2 * k + 1].wait()
        if k == 0:
            c_low = jnp.where(slot < 2, roll(from_left[0], LANES - 2), pc)
            c_high = jnp.where(slot < 2, pc, roll(from_right[0], 2))
        lo, hi, own = from_left[k], from_right[k], pf[k]

        def update(v, factor):
            return v + factor * (across(v) + roll(v, 1) + roll(v, LANES - 1) - 4.0 * v)

        low = update(jnp.where(slot < 2, lo, own), c_low)
        high = update(jnp.where(slot < 2, own, hi), c_high)
        d_one[k] = jnp.where(slot == 1, roll(hi, LANES - 1), roll(lo, 1))
        d_two[k] = jnp.where(slot == 1, roll(high, LANES - 1), roll(low, 1))
        d_q[k] = jnp.where(slot == 1, hi, lo)

        def forward(i, a):
            for u in range(UNROLL):
                j = i * UNROLL + u
                x = k * PACK + j
                back = LANES - 2 - 4 * j
                g = transverse(
                    fv[x] + c_edge * roll(d_one[k], back), roll(d_two[k], back)
                )
                hv[x] = hv[x] + c_edge * roll(d_q[k], back)
                fv[x] = g
                a = root * a + g
                av[x] = a
            return a

        carry = lax.fori_loop(0, PACK // UNROLL, forward, carry)
    sum_low = carry

    def backward(i, carry):
        pull, pull_two, ahead, weight = carry
        for u in range(UNROLL):
            x = m - 1 - (i * UNROLL + u)
            b = root * pull
            w = height * (av[x] + b) + hv[x]
            pull = b + fv[x]
            b_two = root * pull_two
            hv[x] = w
            av[x] = b_two
            pull_two = b_two + w
            ahead = ahead + weight * w
            weight = weight * root
        return pull, pull_two, ahead, weight

    sum_high, twice_high, twice_low, _ = lax.fori_loop(
        0, m // UNROLL, backward, (zero, zero, zero, zero + 1.0)
    )
    same = height**2 * root**2 / (1.0 - root**2)
    cross = height**2 * root ** (m + 1) / (1.0 - root**2)
    planes = (
        (height**2 * sum_low, height * twice_low + same * sum_low + cross * sum_high),
        (height**2 * sum_high, height * twice_high + same * sum_high + cross * sum_low),
    )
    half = parts // 2
    rows = ny // half
    for way in range(2):
        for e in range(half):
            for n in range(2):
                pieces[way * half + e, n] = planes[way][n][e * rows : (e + 1) * rows]

    gathered[me] = pieces[me]
    sends = []
    for o in range(1, parts):
        peer = lax.rem(me + o, parts)
        copy = pltpu.make_async_remote_copy(
            src_ref=pieces.at[peer], dst_ref=gathered.at[me],
            send_sem=s_one.at[o], recv_sem=r_one.at[o],
            device_id={"gy": peer}, device_id_type=pl.DeviceIdType.MESH,
        )
        copy.start()
        sends.append(copy)
    for copy in sends:
        copy.wait()

    from_below = me < half
    for d in range(parts):
        total_u = jnp.zeros((rows, LANES), jnp.float32)
        total_v = total_u
        for e in range(parts):
            down = (d - e) % parts or parts
            up = (e - d) % parts or parts
            by = jnp.where(from_below, near[down], near[up])
            by_far = jnp.where(from_below, far[down], far[up])
            total_u = total_u + by * gathered[e, 0]
            total_v = total_v + by * gathered[e, 1] + by_far * gathered[e, 0]
        mixed[d, 0] = total_u
        mixed[d, 1] = total_v

    incoming[me] = mixed[me]
    sends = []
    for o in range(1, parts):
        peer = lax.rem(me + o, parts)
        copy = pltpu.make_async_remote_copy(
            src_ref=mixed.at[peer], dst_ref=incoming.at[me],
            send_sem=s_two.at[o], recv_sem=r_two.at[o],
            device_id={"gy": peer}, device_id_type=pl.DeviceIdType.MESH,
        )
        copy.start()
        sends.append(copy)

    def finish_local(i, a):
        for u in range(UNROLL):
            x = i * UNROLL + u
            a = root * a + hv[x]
            av[x] = height * (a + av[x]) + qv[x]
        return a

    lax.fori_loop(0, m // UNROLL, finish_local, zero)
    for copy in sends:
        copy.wait()

    low_u, low_v, high_u, high_v = (
        jnp.concatenate([incoming[way * half + e, n] for e in range(half)], axis=0)
        for way in range(2)
        for n in range(2)
    )
    mirror = height**2 * root / (1.0 - root**2)
    low_v = low_v + mirror * sum_high
    high_v = high_v + mirror * sum_low

    def add_high(i, carry):
        u_now, v_now = carry
        for u in range(UNROLL):
            x = m - 1 - (i * UNROLL + u)
            u_now = root * u_now
            v_now = root * v_now + u_now
            av[x] = av[x] + v_now
        return u_now, v_now

    lax.fori_loop(0, m // UNROLL, add_high, (high_u, high_v))

    def add_low(i, carry):
        u_now, v_now = carry
        for u in range(UNROLL):
            x = i * UNROLL + u
            u_now = root * u_now
            v_now = root * v_now + u_now
            out_ref[x] = av[x] + v_now
        return u_now, v_now

    lax.fori_loop(0, m // UNROLL, add_low, (low_u, low_v))


def per_device(field, c, q):
    m, ny, nz = field.shape
    parts = lax.axis_size("gy")
    rings = lax.axis_size("gz")
    assert nz == LANES and m % PACK == 0 and ny % (parts // 2) == 0
    groups = m // PACK
    rows = ny // (parts // 2)
    block = pltpu.VMEM((m, ny, nz), jnp.float32)
    packed = pltpu.VMEM((groups, ny, LANES), jnp.float32)
    small = pltpu.VMEM((parts, 2, rows, LANES), jnp.float32)
    dma = pltpu.SemaphoreType.DMA
    return pl.pallas_call(
        functools.partial(kernel, m, ny, parts, rings),
        out_shape=jax.ShapeDtypeStruct(field.shape, jnp.float32),
        in_specs=[
            pl.BlockSpec(memory_space=pltpu.HBM),
            pl.BlockSpec(memory_space=pltpu.VMEM),
            pl.BlockSpec(memory_space=pltpu.HBM),
        ],
        out_specs=pl.BlockSpec(memory_space=pltpu.VMEM),
        scratch_shapes=[block] * 4 + [packed] * 8 + [small] * 4 + [
            dma((groups,)), dma((groups,)), dma((2, groups)), dma((2, groups)),
            dma((parts,)), dma((parts,)), dma((parts,)), dma((parts,)),
        ],
        compiler_params=pltpu.CompilerParams(
            collective_id=0, has_side_effects=True, vmem_limit_bytes=28 * 2**20
        ),
    )(pltpu.with_memory_space_constraint(field, pltpu.HBM), c, pltpu.with_memory_space_constraint(q, pltpu.HBM))


def solution(mesh):
    placed = (P("gy", None, "gz"), P(None, "gz"), P("gy", None, "gz"))
    return jax.shard_map(
        per_device, mesh=mesh, in_specs=placed, out_specs=P("gy", None, "gz"), check_vma=False
    )
```
